32 devices in a mesh: rep: 2 (over x), zero: 16 (over z, y, core).
Axes of the slice: x: 2, y: 2, z: 4, core: 2. Of those that a mesh axis runs over, the one named last changes fastest.
Arguments:
- gated_input: bfloat16 [2, 2048, 4096], P('rep', 'zero'), may hold values from -6 to 6
- query_gate: bfloat16 [2, 2048, 4096], P('rep', 'zero'), may hold values from -12 to 12
- cotangent: bfloat16 [2, 2048, 4096], P('rep', 'zero'), may hold values from -8 to 8
- filters: float32 [2, 256, 128], P('rep', 'zero'), may hold values from -0.5 to 0.5
- first_moment: float32 [2, 256, 128], P('rep', 'zero'), may hold values from -0.03125 to 0.03125
- second_moment: float32 [2, 256, 128], P('rep', 'zero'), may hold values from 1e-06 to 0.0001
- step_index: int32 [1], replicated, may hold values from 0 to 999
Outputs:
- query_grad: bfloat16 [2, 2048, 4096], P('rep', 'zero')
- input_grad: bfloat16 [2, 2048, 4096], P('rep', 'zero')
- new_filters: float32 [2, 256, 128], P('rep', 'zero')
The draws below stay inside these ranges and needn't reach their ends.
All inputs are finite; a program needn't handle non-finite values.
Results may differ from the reference program's by a relative error of at most 0.007.
Values may be sent and summed in bfloat16 or wider, within the bound.
No kernel may reach another device: no remote copies, remote signals or barrier semaphores. Data moves between devices by JAX's collectives and lax.ppermute only.
A program may use at most 256 MiB of HBM per device.

```python
import math
import jax
import jax.numpy as jnp
from jax import lax

C = 4096
GS = 16
K = 128
G = 256
TOKENS = 2048
REPS = 2
N_REP = 2


def draw_query_gate(key, part):
    channel_pos = jnp.arange(C).astype(jnp.float32) / C
    scale_row = 0.3 * jnp.exp(jnp.log(10.0) * channel_pos)
    base = jnp.clip(jax.random.normal(key, (REPS, TOKENS, C), jnp.float32), -4.0, 4.0)
    return (base * scale_row[None, None, :]).astype(jnp.bfloat16)


def draw_cotangent(key, part):
    position = jnp.arange(TOKENS).astype(jnp.float32) / TOKENS
    scale_col = 0.6 * jnp.exp(jnp.log(3.0) * position)
    base = jnp.clip(jax.random.normal(key, (REPS, TOKENS, C), jnp.float32), -4.0, 4.0)
    return (base * scale_col[None, :, None]).astype(jnp.bfloat16)


def level_of(stream_key, dims, split, low, top_value):
    loudness, own = 1.0, jax.random.fold_in(stream_key, 6)
    for dim, parts in split:
        draws = jnp.exp(jax.random.uniform(jax.random.fold_in(own, dim), (parts,), jnp.float32, low / len(split), top_value / len(split)))
        loudness = loudness * jnp.repeat(draws, dims[dim] // parts).reshape([-1 if axis == dim else 1 for axis in range(len(dims))])
    return loudness


def gaussian(key, shape, scale, limit, cuts=(), held_as=jnp.bfloat16):
    entries = jax.random.normal(key, shape, jnp.float32) * scale
    if len(cuts) > 0:
        entries = level_of(key, shape, cuts, -0.22, 0.18) * entries
    return jnp.clip(entries, min=-limit, max=limit).astype(held_as)


def setup_inputs(seed: int = 0) -> dict:
    keys = jax.random.split(jax.random.key(seed), 8)
    gated_input = gaussian(keys[0], (REPS, TOKENS, C), 1.0, 6.0, ((0, 2), (1, 16)))
    query_gate = draw_query_gate(jax.random.fold_in(keys[7], 71), 0)
    cotangent = draw_cotangent(jax.random.fold_in(keys[7], 71), 0)
    filters = gaussian(keys[3], (REPS, G, K), K ** -0.5, 0.5, ((0, 2), (1, 16)), jnp.float32)
    first_moment = gaussian(keys[4], (REPS, G, K), 0.005, 0.03125, ((0, 2), (1, 16)), jnp.float32)
    second_moment = jnp.clip(jnp.exp(math.log(0.0001) - 4.6051702 * jax.random.uniform(keys[5], (REPS, G, K), jnp.float32) ** level_of(keys[5], (REPS, G, K), ((0, 2), (1, 16)), -0.2, 0.2)), 9.999999974752427e-07, 0.0001)
    step_index = jax.random.randint(keys[6], (1,), 0, 1000).astype(jnp.int32)
    return dict(gated_input=gated_input, query_gate=query_gate, cotangent=cotangent, filters=filters, first_moment=first_moment, second_moment=second_moment, step_index=step_index)


CLIP_NORM = 1.0
BETA_ONE = 0.9
BETA_TWO = 0.95
LEARN_RATE = 0.05
ADAM_EPS = 1e-08

def one_group(operands):
    inputs, gate_values, upstream, filter_row = operands
    length = 2 * TOKENS
    inputs_wide = inputs.astype(jnp.float32)
    upstream_wide = upstream.astype(jnp.float32)
    mixed_half = (upstream_wide * gate_values.astype(jnp.float32)).astype(jnp.bfloat16)
    mixed_half = lax.optimization_barrier(mixed_half)
    mixed_rows = mixed_half.astype(jnp.float32)
    per_channel = jnp.repeat(filter_row.astype(jnp.float32), GS, axis=0).T
    spec_input = jnp.fft.rfft(inputs_wide, length, axis=0)
    spec_filter = jnp.fft.rfft(per_channel, length, axis=0)
    spec_mixed = jnp.fft.rfft(mixed_rows, length, axis=0)
    conv_out = jnp.fft.irfft(spec_input * spec_filter, length, axis=0)[:TOKENS]
    query_grad = (upstream_wide * conv_out).astype(jnp.bfloat16)
    input_grad = jnp.fft.irfft(spec_mixed * jnp.conj(spec_filter), length, axis=0)[:TOKENS].astype(jnp.bfloat16)
    lagged = jnp.fft.irfft(spec_mixed * jnp.conj(spec_input), length, axis=0)[:K]
    grad = lagged.reshape(K, C // GS, GS).sum(axis=2).T
    return (query_grad, input_grad, grad.astype(jnp.float32))

def reference(gated_input, query_gate, cotangent, filters, first_moment, second_moment, step_index):
    half_filters = filters.astype(jnp.bfloat16)
    query_grad, input_grad, grads = lax.map(one_group, (gated_input, query_gate, cotangent, half_filters))
    norm_value = jnp.sqrt(lax.optimization_barrier(jnp.sum(grads * grads, axis=(1, 2))))
    clip_scale = jnp.minimum(1.0, CLIP_NORM / (norm_value + 1e-06))
    clipped = grads * clip_scale[:, None, None]
    step_count = step_index[0].astype(jnp.float32) + 1.0
    moment_one = BETA_ONE * first_moment + (1.0 - BETA_ONE) * clipped
    moment_two = BETA_TWO * second_moment + (1.0 - BETA_TWO) * clipped * clipped
    corrected_one = moment_one / (1.0 - jnp.power(BETA_ONE, step_count))
    corrected_two = moment_two / (1.0 - jnp.power(BETA_TWO, step_count))
    stepped = filters - LEARN_RATE * corrected_one / (jnp.sqrt(corrected_two) + ADAM_EPS)
    bit_count = N_REP.bit_length() - 1
    partner_bit = step_index[0] % bit_count
    partners = jnp.bitwise_xor(jnp.arange(N_REP, dtype=jnp.int32), jnp.left_shift(jnp.int32(1), partner_bit))
    new_filters = 0.5 * (stepped + stepped[partners])
    return (query_grad, input_grad, new_filters)
```

```python
from functools import partial

import jax
import jax.numpy as jnp
from jax import lax
from jax.experimental import pallas as pl
from jax.experimental.pallas import tpu as pltpu
from jax.sharding import PartitionSpec as P

CLIP_NORM = 1.0
BETA_ONE = 0.9
BETA_TWO = 0.95
LEARN_RATE = 0.05
ADAM_EPS = 1e-08

LANES = 128
HALVES = 2


def swapped(value, axis, apart):
    mask = 2**apart
    pairs = [(source, source ^ mask) for source in range(lax.axis_size(axis))]
    return lax.ppermute(value, axis, pairs)


def passed_along(block, axis, distance):
    devices = range(lax.axis_size(axis))
    route = [(i - distance, i) for i in devices if i - distance in devices]
    return lax.ppermute(block, axis, route)


def iota(shape, dim):
    return lax.broadcasted_iota(jnp.int32, shape, dim)


def flip_matrix(size):
    return (iota((size, size), 0) + iota((size, size), 1) == size - 1).astype(jnp.bfloat16)


def dot_f32(lhs, rhs):
    return jnp.dot(lhs, rhs, preferred_element_type=jnp.float32)


def dot_nt(lhs, rhs):
    return lax.dot_general(lhs, rhs, (((1,), (1,)), ((), ())), preferred_element_type=jnp.float32)


def split_halves(block, axis):
    lane = iota(block.shape, 1)
    zero = jnp.zeros_like(block)
    parts = [jnp.where(lane // LANES == half, block, zero) for half in range(HALVES)]
    return jnp.concatenate(parts, axis=axis)


def lag_sums(mixed, source, keep_below, width):
    rows, block_width = mixed.shape
    per_tile = LANES // width
    flipped = dot_f32(flip_matrix(rows), source).astype(jnp.bfloat16)
    rhs = split_halves(flipped, 0)
    chunk = (iota(mixed.shape, 1) % LANES) // width
    zero = jnp.zeros_like(mixed)
    stacked = jnp.concatenate([jnp.where(chunk == q, mixed, zero) for q in range(per_tile)], axis=0)
    lags = dot_nt(stacked, rhs)
    row = iota((rows, rows), 0)
    flipped_col = iota((rows, rows), 1)
    below = row + flipped_col >= rows - 1
    keep = below if keep_below else jnp.logical_not(below)
    sums = []
    for half in range(HALVES):
        for q in range(per_tile):
            part = lags[q * rows : (q + 1) * rows, half * rows : (half + 1) * rows]
            part = jnp.where(keep, part, 0.0)
            turned = pltpu.roll(part, 1, 1, stride=1, stride_axis=0)
            sums.append(jnp.sum(turned, axis=0, keepdims=True))
    return jnp.concatenate(sums, axis=0)


def own_lag_kernel(width, x_ref, gate_ref, up_ref, mixed_ref, lag_ref):
    mixed = (up_ref[...].astype(jnp.float32) * gate_ref[...].astype(jnp.float32)).astype(jnp.bfloat16)
    mixed_ref[...] = mixed
    lag_ref[...] = lag_sums(mixed, x_ref[...], True, width)


def past_lag_kernel(width, mixed_ref, past_ref, lag_ref, grad_ref):
    sums = lag_sums(mixed_ref[...], past_ref[...], False, width)
    grad_ref[...] = (lag_ref[...] + sums).astype(jnp.bfloat16)


def toeplitz_product(filters, own, other, backward, width):
    rows, block_width = own.shape
    per_tile = LANES // width
    row = iota((rows, rows), 0)
    col = iota((rows, rows), 1)
    if backward:
        base = filters.astype(jnp.float32)
        keep = col >= row
    else:
        turn = ((row + col) % rows == 0).astype(jnp.bfloat16)
        base = dot_f32(filters, turn)
        keep = col <= row
    rhs = jnp.concatenate([split_halves(own, 0), split_halves(other, 0)], axis=0)
    zero = jnp.zeros((rows, rows), jnp.bfloat16)
    slabs = []
    for q in range(per_tile):
        tables = []
        for half in range(HALVES):
            g = half * per_tile + q
            line = jnp.broadcast_to(base[g : g + 1, :], (rows, rows))
            tables.append(pltpu.roll(line, 0, 1, stride=1, stride_axis=0).astype(jnp.bfloat16))
        near = [jnp.where(keep, table, zero) for table in tables]
        far = [jnp.where(keep, zero, table) for table in tables]
        slabs.append(jnp.concatenate(near + far, axis=1))
    out = dot_f32(jnp.concatenate(slabs, axis=0), rhs)
    chunk = (iota(own.shape, 1) % LANES) // width
    result = out[:rows]
    for q in range(1, per_tile):
        result = jnp.where(chunk == q, out[q * rows : (q + 1) * rows], result)
    return result


def conv_kernel(width, filter_ref, x_ref, past_ref, up_ref, out_ref):
    conv = toeplitz_product(filter_ref[...], x_ref[...], past_ref[...], False, width)
    out_ref[...] = (up_ref[...].astype(jnp.float32) * conv).astype(jnp.bfloat16)


def back_kernel(width, filter_ref, mixed_ref, next_ref, out_ref):
    back = toeplitz_product(filter_ref[...], mixed_ref[...], next_ref[...], True, width)
    out_ref[...] = back.astype(jnp.bfloat16)


def blockwise(kernel, rows, channels, width, filter_len, kinds, out_kinds, name, flops):
    block = HALVES * LANES
    groups = block // width
    shapes = {"c": (rows, block), "g": (groups, filter_len)}
    specs = {
        "c": pl.BlockSpec(shapes["c"], lambda n: (0, n)),
        "g": pl.BlockSpec(shapes["g"], lambda n: (n, 0)),
    }
    full = {"c": (rows, channels), "g": (channels // width, filter_len)}
    outs = [jax.ShapeDtypeStruct(full[kind], dtype) for kind, dtype in out_kinds]
    return pl.pallas_call(
        partial(kernel, width),
        grid=(channels // block,),
        in_specs=[specs[kind] for kind in kinds],
        out_specs=[specs[kind] for kind, _ in out_kinds],
        out_shape=outs,
        cost_estimate=pl.CostEstimate(flops=flops, transcendentals=0, bytes_accessed=2 * rows * channels * 4),
        name=name,
    )


def gathered(shard, axis):
    full = shard
    index = lax.axis_index(axis)
    for bit in range(lax.axis_size(axis).bit_length() - 1):
        other = swapped(full, axis, bit)
        low = (index >> bit) % 2 == 0
        full = jnp.concatenate([jnp.where(low, full, other), jnp.where(low, other, full)], axis=0)
    return full


def summed(part, axis):
    for bit in range(lax.axis_size(axis).bit_length() - 1):
        other = swapped(part, axis, bit)
        total = part.astype(jnp.float32) + other.astype(jnp.float32)
        part = total.astype(part.dtype)
    return total


def swap_bit(values, bit_number):
    return swapped(values, "rep", bit_number)


def on_device(gated_input, query_gate, cotangent, filters, first_moment, second_moment, step_index):
    inputs = gated_input[0]
    gate_values = query_gate[0]
    upstream = cotangent[0]
    rows, channels = inputs.shape
    filter_len = filters.shape[2]
    shard_len = filters.shape[1]
    groups_all = shard_len * lax.axis_size("zero")
    width = channels // groups_all
    assert rows == filter_len == LANES and LANES % width == 0
    flops = 2 * rows * rows * channels * 2 * 8
    call = partial(blockwise, rows=rows, channels=channels, width=width, filter_len=filter_len, flops=flops)
    bf16, f32 = jnp.bfloat16, jnp.float32

    past_rows = passed_along(inputs, "zero", 1)
    half_filters = gathered(filters[0].astype(bf16), "zero")
    mixed, own_lags = call(own_lag_kernel, kinds="ccc", out_kinds=[("c", bf16), ("g", f32)], name="own_lags")(
        inputs, gate_values, upstream
    )
    next_rows = passed_along(mixed, "zero", -1)
    (local_grad,) = call(past_lag_kernel, kinds="ccg", out_kinds=[("g", bf16)], name="past_lags")(
        mixed, past_rows, own_lags
    )
    grad_full = summed(local_grad, "zero")
    (query_grad,) = call(conv_kernel, kinds="gccc", out_kinds=[("c", bf16)], name="conv")(
        half_filters, inputs, past_rows, upstream
    )
    (input_grad,) = call(back_kernel, kinds="gcc", out_kinds=[("c", bf16)], name="back")(
        half_filters, mixed, next_rows
    )

    total_sq = jnp.sum(grad_full * grad_full)
    grad_shard = lax.dynamic_slice_in_dim(grad_full, lax.axis_index("zero") * shard_len, shard_len, 0)
    clip_scale = jnp.minimum(1.0, CLIP_NORM / (jnp.sqrt(total_sq) + 1e-06))
    clipped = grad_shard * clip_scale
    step_count = step_index[0].astype(jnp.float32) + 1.0
    moment_one = BETA_ONE * first_moment[0] + (1.0 - BETA_ONE) * clipped
    moment_two = BETA_TWO * second_moment[0] + (1.0 - BETA_TWO) * clipped * clipped
    corrected_one = moment_one / (1.0 - jnp.power(BETA_ONE, step_count))
    corrected_two = moment_two / (1.0 - jnp.power(BETA_TWO, step_count))
    stepped = filters[0] - LEARN_RATE * corrected_one / (jnp.sqrt(corrected_two) + ADAM_EPS)
    bit_count = lax.axis_size("rep").bit_length() - 1
    partner_bit = step_index[0] % bit_count
    branches = [partial(swap_bit, bit_number=number) for number in range(bit_count)]
    partner_values = lax.switch(partner_bit, branches, stepped)
    new_filters = 0.5 * (stepped + partner_values)
    return (query_grad[None], input_grad[None], new_filters[None])


def solution(mesh):
    spec = P("rep", "zero", None)
    return jax.shard_map(
        on_device,
        mesh=mesh,
        in_specs=(spec,) * 6 + (P(),),
        out_specs=(spec,) * 3,
        check_vma=False,
    )
```

```python
from functools import partial

import jax
import jax.numpy as jnp
from jax import lax
from jax.experimental import pallas as pl
from jax.experimental.pallas import tpu as pltpu
from jax.sharding import PartitionSpec as P

CLIP_NORM = 1.0
BETA_ONE = 0.9
BETA_TWO = 0.95
LEARN_RATE = 0.05
ADAM_EPS = 1e-08

LANES = 128
TILES = 8


def swapped(value, axis, apart):
    mask = 2**apart
    pairs = [(source, source ^ mask) for source in range(lax.axis_size(axis))]
    return lax.ppermute(value, axis, pairs)


def passed_along(block, axis, distance):
    devices = range(lax.axis_size(axis))
    route = [(i - distance, i) for i in devices if i - distance in devices]
    return lax.ppermute(block, axis, route)


def iota(shape, dim):
    return lax.broadcasted_iota(jnp.int32, shape, dim)


def dot_f32(lhs, rhs):
    return jnp.dot(lhs, rhs, preferred_element_type=jnp.float32)


def dot_nt(lhs, rhs):
    return lax.dot_general(lhs, rhs, (((1,), (1,)), ((), ())), preferred_element_type=jnp.float32)


def turn_matrix(size):
    return ((iota((size, size), 0) + iota((size, size), 1)) % size == 0).astype(jnp.bfloat16)


def windows(ahead, behind):
    both = jnp.concatenate([ahead, behind], axis=0)
    quarter = both.shape[0] // 4
    return jnp.concatenate([both[: 3 * quarter], both[quarter:]], axis=1)


def lane_tiles(*refs):
    for tile in range(refs[0].shape[1] // LANES):
        yield tile, [ref[:, tile * LANES : (tile + 1) * LANES] for ref in refs]


def mix_kernel(width, gate_ref, up_ref, mixed_ref, flipped_ref):
    mixed = (up_ref[...].astype(jnp.float32) * gate_ref[...].astype(jnp.float32)).astype(jnp.bfloat16)
    mixed_ref[...] = mixed
    rows = mixed.shape[0]
    half = rows // 2
    row, col = iota((rows, rows), 0), iota((rows, rows), 1)
    mirror = (row // half == col // half) & (row % half + col % half == half - 1)
    flipped_ref[...] = dot_f32(mirror.astype(jnp.bfloat16), mixed).astype(jnp.bfloat16)


def lag_kernel(width, flipped_ref, x_ref, past_ref, grad_ref, sums_ref):
    per_tile = LANES // width
    rows = x_ref.shape[0]
    half = rows // 2
    step = pl.program_id(0)
    tiles = x_ref.shape[1] // LANES
    chunk = (iota((half, 2 * LANES), 1) % LANES) // width
    near = iota((half, rows), 1) > half - 1 - iota((half, rows), 0)
    for tile, (mixed, x, past) in lane_tiles(flipped_ref, x_ref, past_ref):
        sides = jnp.concatenate([mixed[:half], mixed[half:]], axis=1)
        zero = jnp.zeros_like(sides)
        lhs = jnp.concatenate([jnp.where(chunk == q, sides, zero) for q in range(per_tile)], axis=0)
        rhs = windows(past, x)
        rhs = jnp.concatenate([rhs, rhs[:half]], axis=0)
        lags = dot_nt(lhs, rhs)
        sums = []
        for q in range(per_tile):
            part = lags[q * half : (q + 1) * half]
            part = jnp.where(near, part[:, :rows], part[:, rows:])
            turned = pltpu.roll(part, half + 1, 1, stride=1, stride_axis=0)
            sums.append(jnp.sum(turned, axis=0, keepdims=True))
        start = pl.multiple_of((step * tiles + tile) * per_tile, per_tile)
        sums_ref[pl.ds(start, per_tile), :] = jnp.concatenate(sums, axis=0)

    @pl.when(step == pl.num_programs(0) - 1)
    def _():
        grad_ref[...] = dot_f32(sums_ref[...].astype(jnp.bfloat16), turn_matrix(rows)).astype(jnp.bfloat16)


def toeplitz_product(filters, ahead, behind, backward, width):
    per_tile = LANES // width
    rows = ahead.shape[0]
    half = rows // 2
    row, col = iota((half, rows), 0), iota((half, rows), 1)
    keep = col >= row if backward else col > row
    zero = jnp.zeros((half, rows), jnp.bfloat16)
    slabs = []
    for q in range(per_tile):
        line = jnp.broadcast_to(filters[q : q + 1, :], (half, rows))
        table = pltpu.roll(line, 0, 1, stride=1, stride_axis=0).astype(jnp.bfloat16)
        left = jnp.where(keep, table, zero)
        right = jnp.where(keep, zero, table)
        slabs.append(jnp.concatenate([left, right[:, :half]], axis=1))
    out = dot_f32(jnp.concatenate(slabs, axis=0), windows(ahead, behind))
    chunk = (iota((half, 2 * LANES), 1) % LANES) // width
    result = out[:half]
    for q in range(1, per_tile):
        result = jnp.where(chunk == q, out[q * half : (q + 1) * half], result)
    return jnp.concatenate([result[:, :LANES], result[:, LANES:]], axis=0)


def conv_kernel(width, filter_ref, x_ref, past_ref, up_ref, out_ref, base_ref):
    per_tile = LANES // width
    step = pl.program_id(0)

    @pl.when(step == 0)
    def _():
        base_ref[...] = dot_f32(filter_ref[...], turn_matrix(filter_ref.shape[1]))

    groups = per_tile * (x_ref.shape[1] // LANES)
    base = base_ref[pl.ds(pl.multiple_of(step * groups, groups), groups), :]
    for tile, (x, past, up) in lane_tiles(x_ref, past_ref, up_ref):
        filters = base[tile * per_tile : (tile + 1) * per_tile]
        conv = toeplitz_product(filters, past, x, False, width)
        out_ref[:, tile * LANES : (tile + 1) * LANES] = (up.astype(jnp.float32) * conv).astype(jnp.bfloat16)


def back_kernel(width, filter_ref, mixed_ref, next_ref, out_ref):
    per_tile = LANES // width
    base = filter_ref[...].astype(jnp.float32)
    for tile, (mixed, after) in lane_tiles(mixed_ref, next_ref):
        filters = base[tile * per_tile : (tile + 1) * per_tile]
        back = toeplitz_product(filters, mixed, after, True, width)
        out_ref[:, tile * LANES : (tile + 1) * LANES] = back.astype(jnp.bfloat16)


def blockwise(kernel, kinds, out_kinds, name, rows, channels, width, filter_len, flops, tiles=TILES, scratch=()):
    block = tiles * LANES
    groups = block // width
    full = {"c": (rows, channels), "g": (channels // width, filter_len)}
    full["w"] = full["g"]
    specs = {
        "c": pl.BlockSpec((rows, block), lambda n: (0, n)),
        "g": pl.BlockSpec((groups, filter_len), lambda n: (n, 0)),
        "w": pl.BlockSpec(full["w"], lambda n: (0, 0)),
    }
    return pl.pallas_call(
        partial(kernel, width),
        grid=(channels // block,),
        in_specs=[specs[kind] for kind in kinds],
        out_specs=[specs[kind] for kind, _ in out_kinds],
        out_shape=[jax.ShapeDtypeStruct(full[kind], dtype) for kind, dtype in out_kinds],
        scratch_shapes=[pltpu.VMEM(shape, dtype) for shape, dtype in scratch],
        cost_estimate=pl.CostEstimate(flops=flops, transcendentals=0, bytes_accessed=2 * rows * channels * 4),
        name=name,
    )


def gathered(shard, axis):
    full = shard
    index = lax.axis_index(axis)
    for bit in range(lax.axis_size(axis).bit_length() - 1):
        other = swapped(full, axis, bit)
        low = (index >> bit) % 2 == 0
        full = jnp.concatenate([jnp.where(low, full, other), jnp.where(low, other, full)], axis=0)
    return full


def summed(part, axis):
    for bit in range(lax.axis_size(axis).bit_length() - 1):
        other = swapped(part, axis, bit)
        total = part.astype(jnp.float32) + other.astype(jnp.float32)
        part = total.astype(part.dtype)
    return total


def swap_bit(values, bit_number):
    return swapped(values, "rep", bit_number)


def on_device(gated_input, query_gate, cotangent, filters, first_moment, second_moment, step_index):
    inputs = gated_input[0]
    gate_values = query_gate[0]
    upstream = cotangent[0]
    rows, channels = inputs.shape
    filter_len = filters.shape[2]
    shard_len = filters.shape[1]
    groups_all = shard_len * lax.axis_size("zero")
    width = channels // groups_all
    assert rows == filter_len == LANES and LANES % width == 0
    flops = 2 * rows * rows * channels * 8
    call = partial(blockwise, rows=rows, channels=channels, width=width, filter_len=filter_len, flops=flops)
    bf16, f32 = jnp.bfloat16, jnp.float32

    past_rows = passed_along(inputs, "zero", 1)
    half_filters = gathered(filters[0].astype(bf16), "zero")
    mixed, flipped = call(mix_kernel, kinds="cc", out_kinds=[("c", bf16), ("c", bf16)], name="mix")(
        gate_values, upstream
    )
    next_rows = passed_along(mixed, "zero", -1)
    (local_grad,) = call(
        lag_kernel, kinds="ccc", out_kinds=[("w", bf16)], name="lags", scratch=[((groups_all, filter_len), f32)]
    )(flipped, inputs, past_rows)
    grad_full = summed(local_grad, "zero")
    (query_grad,) = call(conv_kernel, kinds="wccc", out_kinds=[("c", bf16)], name="conv", scratch=[((groups_all, filter_len), f32)])(
        half_filters, inputs, past_rows, upstream
    )
    (input_grad,) = call(back_kernel, kinds="gcc", out_kinds=[("c", bf16)], name="back")(
        half_filters, mixed, next_rows
    )

    total_sq = jnp.sum(grad_full * grad_full)
    grad_shard = lax.dynamic_slice_in_dim(grad_full, lax.axis_index("zero") * shard_len, shard_len, 0)
    clip_scale = jnp.minimum(1.0, CLIP_NORM / (jnp.sqrt(total_sq) + 1e-06))
    clipped = grad_shard * clip_scale
    step_count = step_index[0].astype(jnp.float32) + 1.0
    moment_one = BETA_ONE * first_moment[0] + (1.0 - BETA_ONE) * clipped
    moment_two = BETA_TWO * second_moment[0] + (1.0 - BETA_TWO) * clipped * clipped
    corrected_one = moment_one / (1.0 - jnp.power(BETA_ONE, step_count))
    corrected_two = moment_two / (1.0 - jnp.power(BETA_TWO, step_count))
    stepped = filters[0] - LEARN_RATE * corrected_one / (jnp.sqrt(corrected_two) + ADAM_EPS)
    bit_count = lax.axis_size("rep").bit_length() - 1
    partner_bit = step_index[0] % bit_count
    branches = [partial(swap_bit, bit_number=number) for number in range(bit_count)]
    partner_values = lax.switch(partner_bit, branches, stepped)
    new_filters = 0.5 * (stepped + partner_values)
    return (query_grad[None], input_grad[None], new_filters[None])


def solution(mesh):
    spec = P("rep", "zero", None)
    return jax.shard_map(
        on_device,
        mesh=mesh,
        in_specs=(spec,) * 6 + (P(),),
        out_specs=(spec,) * 3,
        check_vma=False,
    )
```
